128 devices in a mesh: gx: 8 (over z, y_lo), gy: 16 (over x, y_hi, core).
Axes of the slice: x: 4, y: 4 (y_hi: 2, y_lo: 2; y = y_hi * 2 + y_lo), z: 4, core: 2. Of those that a mesh axis runs over, the one named last changes fastest.
Arguments:
- velocity: float32 [3, 16, 1024, 2048], P(None, None, 'gx', 'gy'), may hold values from -6 to 6
- metric_first: float32 [2048], P('gy'), may hold values from 0.5 to 2
- metric_curve: float32 [2048], P('gy'), may hold values from -1 to 1
Outputs:
- tendency: float32 [3, 16, 1024, 2048], P(None, None, 'gx', 'gy')
The draws below stay inside these ranges and needn't reach their ends.
All inputs are finite; a program needn't handle non-finite values.
Results may differ from the reference program's by a relative error of at most 0.0003.
Values sent between devices are 32-bit elements; how exact they have to be, the bound alone decides.
No kernel may reach another device: no remote copies, remote signals or barrier semaphores. Data moves between devices by JAX's collectives and lax.ppermute only.
A program may use at most 192 MiB of HBM per device.

```python
import math
import jax
import jax.numpy as jnp
import numpy as np
from jax import lax

KZ = 16
NX = 1024
NY = 2048


def block_levels(stream_key, dims, pieces, least, largest):
    def one(position, parts):
        draws = jax.random.uniform(jax.random.fold_in(jax.random.fold_in(stream_key, 6), position), (parts,), jnp.float32, least / len(pieces), largest / len(pieces))
        return jnp.repeat(jnp.exp(draws), dims[position] // parts).reshape((-1,) + (1,) * (len(dims) - position - 1))

    factor_of = one(*pieces[0])
    for cut in pieces[1:]:
        factor_of = factor_of * one(*cut)
    return factor_of


def gaussian(rng, extent, spread, limit, split=(), kind=jnp.bfloat16):
    level = block_levels(rng, extent, split, -0.22, 0.18) if split else 1.0
    entries = jax.random.normal(rng, extent, jnp.float32) * spread * level
    return jnp.minimum(jnp.maximum(entries, -limit), limit).astype(kind)


def setup_inputs(seed: int = 0) -> dict:
    streams_of = jax.random.split(jax.random.key(seed), 4)
    velocity = gaussian(streams_of[0], (3, KZ, NX, NY), 1.0, 6.0, ((2, 8), (3, 16)), jnp.float32)
    metric_first = jnp.clip(jnp.exp(math.log(2.0) - 1.3862944 * jax.random.uniform(streams_of[1], (NY,), jnp.float32) ** block_levels(streams_of[1], (NY,), ((0, 16),), -0.2, 0.2)), 0.5, 2.0)
    metric_curve = jnp.clip(jax.random.uniform(streams_of[2], (NY,), jnp.float32, -1.0, 1.0) * block_levels(streams_of[2], (NY,), ((0, 16),), -0.4, 0.0), -1.0, 1.0)
    return {"velocity": velocity, "metric_first": metric_first, "metric_curve": metric_curve}


VISCOSITY = 0.1

def stencil_pair(padded, axis, count):

    def shifted(offset):
        return lax.slice_in_dim(padded, 2 + offset, 2 + offset + count, axis=axis)
    centre = shifted(0)
    first = 7.0 / 9.0 * (shifted(1) - shifted(-1)) + 1.0 / 36.0 * (shifted(2) - shifted(-2))
    second = 12.0 / 11.0 * (shifted(1) - 2.0 * centre + shifted(-1)) + 3.0 / 44.0 * (shifted(2) - 2.0 * centre + shifted(-2))
    return (first, second)

def wall_rows(first, second, field, at_low, at_high):
    low_first0 = -2.5 * field[..., 0] + 2.0 * field[..., 1] + 0.5 * field[..., 2]
    low_first1 = 0.75 * (field[..., 2] - field[..., 0])
    high_first_prev = 0.75 * (field[..., -1] - field[..., -3])
    high_first_last = 2.5 * field[..., -1] - 2.0 * field[..., -2] - 0.5 * field[..., -3]
    low_second0 = 2.0 * field[..., 0] - 5.0 * field[..., 1] + 4.0 * field[..., 2] - field[..., 3]
    low_second1 = 1.2 * (field[..., 2] - 2.0 * field[..., 1] + field[..., 0])
    high_second_prev = 1.2 * (field[..., -1] - 2.0 * field[..., -2] + field[..., -3])
    high_second_last = 2.0 * field[..., -1] - 5.0 * field[..., -2] + 4.0 * field[..., -3] - field[..., -4]
    first = first.at[..., 0].set(jnp.where(at_low, low_first0, first[..., 0]))
    first = first.at[..., 1].set(jnp.where(at_low, low_first1, first[..., 1]))
    first = first.at[..., -2].set(jnp.where(at_high, high_first_prev, first[..., -2]))
    first = first.at[..., -1].set(jnp.where(at_high, high_first_last, first[..., -1]))
    second = second.at[..., 0].set(jnp.where(at_low, low_second0, second[..., 0]))
    second = second.at[..., 1].set(jnp.where(at_low, low_second1, second[..., 1]))
    second = second.at[..., -2].set(jnp.where(at_high, high_second_prev, second[..., -2]))
    second = second.at[..., -1].set(jnp.where(at_high, high_second_last, second[..., -1]))
    return (first, second)

def coefficients(total, order, periodic):
    alpha = 1.0 / 3.0 if order == 0 else 2.0 / 11.0
    lower = np.full(total, alpha)
    upper = np.full(total, alpha)
    if not periodic:
        end_coef = 2.0 if order == 0 else 0.0
        near = 0.25 if order == 0 else 0.1
        lower[0] = 0.0
        upper[0] = end_coef
        lower[1] = near
        upper[1] = near
        lower[total - 2] = near
        upper[total - 2] = near
        lower[total - 1] = end_coef
        upper[total - 1] = 0.0
    return (lower, upper)

def x_pair(component):
    spectrum = jnp.fft.rfft(component, axis=1)
    waves = 2.0 * math.pi * jnp.arange(NX // 2 + 1, dtype=jnp.float32) / NX
    transfer_first = (14.0 / 9.0 * jnp.sin(waves) + 1.0 / 18.0 * jnp.sin(2.0 * waves)) / (1.0 + 2.0 / 3.0 * jnp.cos(waves))
    transfer_second = (24.0 / 11.0 * (jnp.cos(waves) - 1.0) + 3.0 / 22.0 * (jnp.cos(2.0 * waves) - 1.0)) / (1.0 + 4.0 / 11.0 * jnp.cos(waves))
    first = jnp.fft.irfft(spectrum * (1j * transfer_first)[None, :, None], n=NX, axis=1)
    second = jnp.fft.irfft(spectrum * transfer_second[None, :, None], n=NX, axis=1)
    return (first.astype(component.dtype), second.astype(component.dtype))

def y_pair(component):
    padded = jnp.pad(component, ((0, 0), (0, 0), (2, 2)))
    first, second = stencil_pair(padded, 2, NY)
    first, second = wall_rows(first, second, component, True, True)
    results = []
    for order, right in ((0, first), (1, second)):
        lower, upper = coefficients(NY, order, False)
        lower_diag = jnp.asarray(lower, jnp.float32)
        upper_diag = jnp.asarray(upper, jnp.float32)
        main_diag = jnp.ones((NY,), jnp.float32)
        columns = right.reshape(-1, NY).T
        solved = lax.linalg.tridiagonal_solve(lower_diag, main_diag, upper_diag, columns)
        results.append(solved.T.reshape(right.shape))
    return (results[0], results[1])

def reference(velocity, metric_first, metric_curve):
    stream = velocity[0]
    normal = velocity[1]

    def one(component):
        dx1, dx2 = x_pair(component)
        first_y, second_y = y_pair(component)
        dy1 = metric_first * first_y
        dy2 = metric_first * metric_first * second_y + metric_curve * first_y
        return -(stream * dx1 + normal * dy1) + VISCOSITY * (dx2 + dy2)
    return lax.map(one, velocity)
```

```python
import functools

import jax
import jax.numpy as jnp
import numpy as np
from jax import lax
from jax.experimental import pallas as pl
from jax.experimental.pallas import tpu as pltpu
from jax.sharding import PartitionSpec as P

VISCOSITY = 0.1
F32 = jnp.float32
BF16 = jnp.bfloat16
GROUP = 8
KINDS = 3
EDGES = 2 * KINDS * GROUP


def coefficients(total, order, walls):
    alpha = 1.0 / 3.0 if order == 0 else 2.0 / 11.0
    lower = np.full(total, alpha)
    upper = np.full(total, alpha)
    lower[0] = 0.0
    upper[total - 1] = 0.0
    if walls:
        end = 2.0 if order == 0 else 0.0
        near = 0.25 if order == 0 else 0.1
        upper[0] = end
        lower[total - 1] = end
        for row in (1, total - 2):
            lower[row] = near
            upper[row] = near
    return lower, upper


def stencil_matrix(total, order, walls):
    matrix = np.zeros((total, total))
    if order == 0:
        taps = {1: 7.0 / 9.0, -1: -7.0 / 9.0, 2: 1.0 / 36.0, -2: -1.0 / 36.0}
    else:
        near, far = 12.0 / 11.0, 3.0 / 44.0
        taps = {0: -2.0 * (near + far), 1: near, -1: near, 2: far, -2: far}
    for offset, value in taps.items():
        rows = np.arange(max(0, -offset), total - max(0, offset))
        matrix[rows, rows + offset] = value
    if walls:
        matrix[[0, 1, -2, -1]] = 0.0
        if order == 0:
            matrix[0, :3] = [-2.5, 2.0, 0.5]
            matrix[1, :3] = [-0.75, 0.0, 0.75]
            matrix[-2, -3:] = [-0.75, 0.0, 0.75]
            matrix[-1, -3:] = [-0.5, -2.0, 2.5]
        else:
            matrix[0, :4] = [2.0, -5.0, 4.0, -1.0]
            matrix[1, :3] = [1.2, -2.4, 1.2]
            matrix[-2, -3:] = [1.2, -2.4, 1.2]
            matrix[-1, -4:] = [-1.0, 4.0, -5.0, 2.0]
    return matrix


class Inverse:
    def __init__(self, lower, upper):
        total = len(lower)
        self.down = np.zeros(total + 1)
        self.up = np.zeros(total + 1)
        low = np.zeros(total + 1)
        for i in range(total - 1, -1, -1):
            low[i] = lower[i] / (1.0 - upper[i] * low[i + 1])
        high = np.zeros(total + 1)
        for i in range(total):
            high[i] = upper[i] / (1.0 - lower[i] * high[i - 1])
        self.down[:total] = -low[:total]
        self.up[:total] = -high[:total]
        self.diagonal = np.array(
            [1.0 / (1.0 - lower[i] * high[i - 1] - upper[i] * low[i + 1]) for i in range(total)]
        )

    def column(self, j, first, last):
        values = np.zeros(last - first)
        value = self.diagonal[j]
        if first <= j < last:
            values[j - first] = value
        for i in range(j + 1, last):
            value = value * self.down[i]
            if i >= first:
                values[i - first] = value
        value = self.diagonal[j]
        for i in range(j - 1, first - 1, -1):
            value = value * self.up[i]
            if i < last:
                values[i - first] = value
        return values


def block_operator(total, order, walls, start, rows):
    lower, upper = coefficients(total, order, walls)
    inverse = Inverse(lower, upper)
    stencil = stencil_matrix(total, order, walls)
    stop = start + rows
    first, last = max(0, start - 2), min(total, stop + 2)
    columns = np.stack([inverse.column(j, start, stop) for j in range(first, last)], axis=1)
    own = columns @ stencil[first:last, start:stop]
    from_low = np.zeros((KINDS, rows))
    from_high = np.zeros((KINDS, rows))
    to_high = np.zeros(rows)
    to_low = np.zeros(rows)
    if start > 0:
        weight = np.cumprod(inverse.down[start:stop])
        from_low[1 + order] = weight
        beyond = inverse.diagonal[start + 1] / weight[1]
        gap = inverse.diagonal[start + 1] * inverse.up[start] - weight[0] * beyond
        from_low[0, 0] = gap * stencil[start + 1, start - 1]
        row = row_of(lower, upper, start, start, stop)
        weight = np.array([inverse.up[start - 1], inverse.up[start - 1] * inverse.up[start - 2]])
        q = np.concatenate(
            [
                [inverse.diagonal[start - 2] / weight[1], inverse.diagonal[start - 1] / weight[0]],
                row,
                row_of(lower, upper, start, stop, min(total, stop + 2)),
            ]
        )
        to_low = q @ stencil[start - 2 : min(total, stop + 2), start:stop]
    if stop < total:
        weight = np.cumprod(inverse.up[start:stop][::-1])[::-1]
        from_high[1 + order] = weight
        beyond = inverse.diagonal[stop - 2] / weight[-2]
        gap = inverse.diagonal[stop - 2] * inverse.down[stop - 1] - weight[-1] * beyond
        from_high[0, -1] = gap * stencil[stop - 2, stop]
        row = row_of(lower, upper, stop - 1, max(0, start - 2), stop)
        weight = np.array([inverse.down[stop], inverse.down[stop] * inverse.down[stop + 1]])
        v = np.concatenate(
            [row, [inverse.diagonal[stop] / weight[0], inverse.diagonal[stop + 1] / weight[1]]]
        )
        to_high = v @ stencil[max(0, start - 2) : stop + 2, start:stop]
    return own, from_low, from_high, to_high, to_low


def row_of(lower, upper, i, first, last):
    turned = Inverse(np.append(0.0, upper[:-1]), np.append(lower[1:], 0.0))
    return turned.column(i, first, last)


def line_tables(total, walls, start, rows, even):
    orders = [block_operator(total, order, walls, start, rows) for order in (0, 1)]
    own = np.stack([item[0] for item in orders])
    low = np.stack([item[1] for item in orders])
    high = np.stack([item[2] for item in orders])
    edge_high = np.zeros(rows)
    edge_high[-1] = 1.0
    edge_low = np.zeros(rows)
    edge_low[0] = 1.0
    to_high = np.stack([edge_high, orders[0][3], orders[1][3]])
    to_low = np.stack([edge_low, orders[0][4], orders[1][4]])
    received = np.concatenate([high, low] if even else [low, high], axis=1)
    sent = np.concatenate([to_high, to_low] if even else [to_low, to_high])
    return own, np.repeat(received, GROUP, axis=1), np.repeat(sent, GROUP, axis=0)


def halves(values):
    high = values.astype(BF16)
    low = (values - high.astype(np.float64)).astype(BF16)
    return high, low


def split(values):
    high = values.astype(BF16)
    low = (values - high.astype(F32)).astype(BF16)
    return high, low


def sum_rows(stacked, concatenate):
    half = EDGES // 2
    return concatenate([stacked[GROUP:half], stacked[half + GROUP :]])


def x_tables(rows):
    sums, mains = [], []
    for even in (True, False):
        own, received, sent = line_tables(5 * rows, False, 2 * rows, rows, even)
        scale = np.array([-1.0, VISCOSITY])[:, None, None]
        high, low = halves((own * scale).reshape(2 * rows, rows))
        edge, rest = halves((received * scale).transpose(1, 0, 2).reshape(EDGES, 2 * rows))
        edge = np.concatenate([edge, edge, sum_rows(rest, np.concatenate)]).T
        mains.append(np.concatenate([high, high, low, edge], axis=1))
        high, low = halves(sent)
        sums.append(
            np.concatenate(
                [np.concatenate([high, high], axis=1), np.concatenate([low, 0 * low], axis=1)]
            )
        )
    return np.stack(sums), np.stack(mains)


def y_tables(parts, rows):
    sums, mains, edges = [], [], []
    for part, even in ((0, True), (2, True), (3, False), (parts - 1, False)):
        own, received, sent = line_tables(parts * rows, True, part * rows, rows, even)
        mains.append(np.concatenate([own[0].T, own[1].T], axis=1))
        edges.append(np.concatenate([received[0], received[1]], axis=1))
        if part in (0, parts - 1):
            continue
        high, low = halves(sent)
        pad = np.zeros((rows // 2 - EDGES, 2 * rows), high.dtype)
        sums.append(
            np.concatenate(
                [
                    np.concatenate([high, high], axis=1),
                    pad,
                    np.concatenate([low, 0 * low], axis=1),
                    pad,
                ]
            ).T
        )
    return np.stack(sums), np.stack(mains).astype(np.float32), np.stack(edges).astype(np.float32)


def edge_kernel(
    chunk,
    field_hbm,
    x_hbm,
    y_hbm,
    x_main_hbm,
    y_main_hbm,
    y_edge_hbm,
    x1_ref,
    x2_ref,
    y1_ref,
    y2_ref,
    field_ref,
    x_main_ref,
    y_main_ref,
    y_edge_ref,
    x_ref,
    y_ref,
    x_acc,
    y_acc,
    field_sems,
    table_sems,
):
    parts, planes, rows, _ = field_ref.shape
    x_odd = lax.axis_index("gx") % 2
    y_index = lax.axis_index("gy")
    y_odd = y_index % 2
    last = lax.axis_size("gy") - 1
    kind = jnp.where(y_index == 0, 0, jnp.where(y_index == last, 3, 1 + y_odd))

    def fetch(i):
        place = pl.ds(i * chunk, chunk)
        return pltpu.make_async_copy(
            field_hbm.at[:, place], field_ref.at[:, place], field_sems.at[i]
        )

    sums = [
        pltpu.make_async_copy(x_hbm.at[x_odd], x_ref, table_sems.at[3]),
        pltpu.make_async_copy(y_hbm.at[y_odd], y_ref, table_sems.at[4]),
    ]
    for copy in sums:
        copy.start()
    steps = planes // chunk
    for i in range(steps):
        fetch(i).start()
    tables = [
        pltpu.make_async_copy(x_main_hbm.at[x_odd], x_main_ref, table_sems.at[0]),
        pltpu.make_async_copy(y_main_hbm.at[kind], y_main_ref, table_sems.at[1]),
        pltpu.make_async_copy(y_edge_hbm.at[kind], y_edge_ref, table_sems.at[2]),
    ]
    for copy in tables:
        copy.start()

    x_row = lax.broadcasted_iota(jnp.int32, (EDGES, rows), 0) % GROUP
    y_lane = lax.broadcasted_iota(jnp.int32, (rows, rows), 1) % GROUP
    half = EDGES // 2
    for copy in sums:
        copy.wait()

    def body(i, carry):
        fetch(i).wait()
        base = lax.rem(i * chunk, GROUP)
        for part in range(parts):
            for z in range(chunk):
                high, low = split(field_ref[part, i * chunk + z])
                place = base + z
                sums = jnp.dot(
                    x_ref[...],
                    jnp.concatenate([high, low], axis=0),
                    preferred_element_type=F32,
                )
                sums = sums[:EDGES] + sums[EDGES:]
                x_acc[part] = jnp.where(x_row == place, sums, x_acc[part])
                sums = jnp.dot(
                    jnp.concatenate([high, low], axis=1),
                    y_ref[...],
                    preferred_element_type=F32,
                )
                y_acc[part] = jnp.where(y_lane == place, sums, y_acc[part])

        @pl.when(base + chunk == GROUP)
        def _():
            start = pl.multiple_of(i * chunk + chunk - GROUP, GROUP)
            target = pl.ds(start, GROUP)
            for part in range(parts):
                values = x_acc[part]
                turned = y_acc[part].T
                turned = turned[:EDGES] + turned[rows // 2 : rows // 2 + EDGES]
                for kind in range(KINDS):
                    near = slice(kind * GROUP, (kind + 1) * GROUP)
                    far = slice(half + kind * GROUP, half + (kind + 1) * GROUP)
                    x1_ref[kind, part, target] = values[near]
                    x2_ref[kind, part, target] = values[far]
                    y1_ref[kind, part, target] = turned[near]
                    y2_ref[kind, part, target] = turned[far]

        return carry

    lax.fori_loop(0, steps, body, 0)
    for copy in tables:
        copy.wait()


def stack_edges(first_ref, second_ref, part, group):
    place = pl.ds(pl.multiple_of(group * GROUP, GROUP), GROUP)
    values = jnp.concatenate(
        [ref[kind, part, place] for ref in (first_ref, second_ref) for kind in range(KINDS)]
    )
    high = values.astype(BF16).astype(F32)
    return jnp.concatenate([high, values - high, sum_rows(high, jnp.concatenate)])


def wall_normal_kernel(
    depth, field_ref, first_ref, second_ref, main_ref, edge_ref, m_ref, curve_ref, out_ref, w_ref
):
    parts, planes, rows, _ = field_ref.shape
    m = m_ref[...]
    curve = curve_ref[...]

    def scaled(table):
        one = table[:, :rows]
        two = table[:, rows:]
        return jnp.concatenate([one * -m, VISCOSITY * (two * (m * m) + one * curve)], axis=1)

    high, low = split(scaled(main_ref[...]))
    edge, rest = split(scaled(edge_ref[...]))
    rest = sum_rows(rest, jnp.concatenate)
    w_ref[...] = jnp.concatenate([high, high, low, edge, edge, rest])
    lane = lax.broadcasted_iota(jnp.int32, (rows, rows), 1) % GROUP

    def body(i, carry):
        start = i * depth
        base = lax.rem(start, GROUP)
        blocks = []
        for part in range(parts):
            edges = stack_edges(first_ref, second_ref, part, start // GROUP).T
            for z in range(depth):
                high, low = split(field_ref[part, start + z])
                edge = jnp.where(lane == base + z, edges, 0.0).astype(BF16)
                blocks.append(jnp.concatenate([high, low, high, edge], axis=1))
        sums = jnp.dot(jnp.concatenate(blocks), w_ref[...], preferred_element_type=F32)
        for part in range(parts):
            for z in range(depth):
                piece = sums[(part * depth + z) * rows : (part * depth + z + 1) * rows]
                normal = field_ref[1, start + z]
                out_ref[part, start + z] = normal * piece[:, :rows] + piece[:, rows:]
        return carry

    lax.fori_loop(0, planes // depth, body, 0)


def streamwise_kernel(depth, field_ref, first_ref, second_ref, main_ref, add_ref, out_ref):
    parts, _, rows, _ = field_ref.shape
    start = pl.program_id(0) * depth
    base = lax.rem(start, GROUP)
    row = lax.broadcasted_iota(jnp.int32, (rows, rows), 0) % GROUP
    for part in range(parts):
        edges = stack_edges(first_ref, second_ref, part, start // GROUP)
        blocks = []
        for z in range(depth):
            high, low = split(field_ref[part, start + z])
            edge = jnp.where(row == base + z, edges, 0.0).astype(BF16)
            blocks.append(jnp.concatenate([high, low, high, edge]))
        sums = jnp.dot(
            main_ref[...], jnp.concatenate(blocks, axis=1), preferred_element_type=F32
        )
        for z in range(depth):
            piece = sums[:, z * rows : (z + 1) * rows]
            out_ref[part, z] = (
                field_ref[0, start + z] * piece[:rows] + piece[rows:] + add_ref[part, start + z]
            )


def exchange(first, second, axis, count, periodic):
    pairs = [(i, i + 1) for i in range(0, count, 2)]
    first = lax.ppermute(first, axis, [p for a, b in pairs for p in ((a, b), (b, a))])
    pairs = [(i, (i + 1) % count) for i in range(1, count if periodic else count - 1, 2)]
    second = lax.ppermute(second, axis, [p for a, b in pairs for p in ((a, b), (b, a))])
    return first, second


CHUNK = 2
DEPTH = 8


def on_device(x_parts, y_parts, velocity, metric_first, metric_curve):
    parts, planes, rows, _ = velocity.shape
    x_sums, x_main = x_tables(rows)
    y_sums, y_main, y_edge = y_tables(y_parts, rows)
    vmem = pl.BlockSpec(memory_space=pltpu.VMEM)
    outside = pl.BlockSpec(memory_space=pltpu.HBM)
    edge_shape = jax.ShapeDtypeStruct((KINDS, parts, planes, rows), F32)

    def on_chip(shape, dtype):
        return pltpu.VMEM(shape, dtype)

    in_specs = [outside] * 6
    x1, x2, y1, y2, field, x_main, y_main, y_edge = pl.pallas_call(
        functools.partial(edge_kernel, CHUNK),
        out_shape=[edge_shape] * 4
        + [
            on_chip(velocity.shape, F32),
            on_chip(x_main.shape[1:], BF16),
            on_chip(y_main.shape[1:], F32),
            on_chip(y_edge.shape[1:], F32),
        ],
        in_specs=in_specs,
        out_specs=[vmem] * 8,
        scratch_shapes=[
            pltpu.VMEM(x_sums.shape[1:], BF16),
            pltpu.VMEM(y_sums.shape[1:], BF16),
            pltpu.VMEM((parts, EDGES, rows), F32),
            pltpu.VMEM((parts, rows, rows), F32),
            pltpu.SemaphoreType.DMA((planes // CHUNK,)),
            pltpu.SemaphoreType.DMA((5,)),
        ],
        compiler_params=pltpu.CompilerParams(vmem_limit_bytes=16 << 20),
        name="edges",
    )(*[
        pltpu.with_memory_space_constraint(item, pltpu.HBM)
        for item in (velocity, x_sums, y_sums, x_main, y_main, y_edge)
    ])

    y1, y2 = exchange(y1, y2, "gy", y_parts, False)
    x1, x2 = exchange(x1, x2, "gx", x_parts, True)

    params = pltpu.CompilerParams(vmem_limit_bytes=16 << 20)
    partial = pl.pallas_call(
        functools.partial(wall_normal_kernel, DEPTH),
        out_shape=on_chip(velocity.shape, F32),
        in_specs=[vmem] * 7,
        out_specs=vmem,
        scratch_shapes=[pltpu.VMEM((4 * rows, 2 * rows), BF16)],
        compiler_params=params,
        name="wall_normal",
    )(field, y1, y2, y_main, y_edge, metric_first[None], metric_curve[None])

    return pl.pallas_call(
        functools.partial(streamwise_kernel, DEPTH),
        out_shape=jax.ShapeDtypeStruct(velocity.shape, F32),
        grid=(planes // DEPTH,),
        in_specs=[vmem] * 5,
        out_specs=pl.BlockSpec((parts, DEPTH, rows, rows), lambda i: (0, i, 0, 0)),
        compiler_params=params,
        name="streamwise",
    )(field, x1, x2, x_main, partial)


def solution(mesh):
    placed = (P(None, None, "gx", "gy"), P("gy"), P("gy"))
    return jax.shard_map(
        functools.partial(on_device, mesh.shape["gx"], mesh.shape["gy"]),
        mesh=mesh,
        in_specs=placed,
        out_specs=P(None, None, "gx", "gy"),
        check_vma=False,
    )
```

```python
import functools

import jax
import jax.numpy as jnp
import numpy as np
from jax import lax
from jax.experimental import pallas as pl
from jax.experimental.pallas import tpu as pltpu
from jax.sharding import PartitionSpec as P

VISCOSITY = 0.1
F32 = jnp.float32
BF16 = jnp.bfloat16
GROUP = 8
KINDS = 3
EDGES = 2 * KINDS * GROUP


def coefficients(total, order, walls):
    alpha = 1.0 / 3.0 if order == 0 else 2.0 / 11.0
    lower = np.full(total, alpha)
    upper = np.full(total, alpha)
    lower[0] = 0.0
    upper[total - 1] = 0.0
    if walls:
        end = 2.0 if order == 0 else 0.0
        near = 0.25 if order == 0 else 0.1
        upper[0] = end
        lower[total - 1] = end
        for row in (1, total - 2):
            lower[row] = near
            upper[row] = near
    return lower, upper


def stencil_matrix(total, order, walls):
    matrix = np.zeros((total, total))
    if order == 0:
        taps = {1: 7.0 / 9.0, -1: -7.0 / 9.0, 2: 1.0 / 36.0, -2: -1.0 / 36.0}
    else:
        near, far = 12.0 / 11.0, 3.0 / 44.0
        taps = {0: -2.0 * (near + far), 1: near, -1: near, 2: far, -2: far}
    for offset, value in taps.items():
        rows = np.arange(max(0, -offset), total - max(0, offset))
        matrix[rows, rows + offset] = value
    if walls:
        matrix[[0, 1, -2, -1]] = 0.0
        if order == 0:
            matrix[0, :3] = [-2.5, 2.0, 0.5]
            matrix[1, :3] = [-0.75, 0.0, 0.75]
            matrix[-2, -3:] = [-0.75, 0.0, 0.75]
            matrix[-1, -3:] = [-0.5, -2.0, 2.5]
        else:
            matrix[0, :4] = [2.0, -5.0, 4.0, -1.0]
            matrix[1, :3] = [1.2, -2.4, 1.2]
            matrix[-2, -3:] = [1.2, -2.4, 1.2]
            matrix[-1, -4:] = [-1.0, 4.0, -5.0, 2.0]
    return matrix


class Inverse:
    def __init__(self, lower, upper):
        total = len(lower)
        self.down = np.zeros(total + 1)
        self.up = np.zeros(total + 1)
        low = np.zeros(total + 1)
        for i in range(total - 1, -1, -1):
            low[i] = lower[i] / (1.0 - upper[i] * low[i + 1])
        high = np.zeros(total + 1)
        for i in range(total):
            high[i] = upper[i] / (1.0 - lower[i] * high[i - 1])
        self.down[:total] = -low[:total]
        self.up[:total] = -high[:total]
        self.diagonal = np.array(
            [1.0 / (1.0 - lower[i] * high[i - 1] - upper[i] * low[i + 1]) for i in range(total)]
        )

    def column(self, j, first, last):
        values = np.zeros(last - first)
        value = self.diagonal[j]
        if first <= j < last:
            values[j - first] = value
        for i in range(j + 1, last):
            value = value * self.down[i]
            if i >= first:
                values[i - first] = value
        value = self.diagonal[j]
        for i in range(j - 1, first - 1, -1):
            value = value * self.up[i]
            if i < last:
                values[i - first] = value
        return values


def block_operator(total, order, walls, start, rows):
    lower, upper = coefficients(total, order, walls)
    inverse = Inverse(lower, upper)
    stencil = stencil_matrix(total, order, walls)
    stop = start + rows
    first, last = max(0, start - 2), min(total, stop + 2)
    columns = np.stack([inverse.column(j, start, stop) for j in range(first, last)], axis=1)
    own = columns @ stencil[first:last, start:stop]
    from_low = np.zeros((KINDS, rows))
    from_high = np.zeros((KINDS, rows))
    to_high = np.zeros(rows)
    to_low = np.zeros(rows)
    if start > 0:
        weight = np.cumprod(inverse.down[start:stop])
        from_low[1 + order] = weight
        beyond = inverse.diagonal[start + 1] / weight[1]
        gap = inverse.diagonal[start + 1] * inverse.up[start] - weight[0] * beyond
        from_low[0, 0] = gap * stencil[start + 1, start - 1]
        row = row_of(lower, upper, start, start, stop)
        weight = np.array([inverse.up[start - 1], inverse.up[start - 1] * inverse.up[start - 2]])
        q = np.concatenate(
            [
                [inverse.diagonal[start - 2] / weight[1], inverse.diagonal[start - 1] / weight[0]],
                row,
                row_of(lower, upper, start, stop, min(total, stop + 2)),
            ]
        )
        to_low = q @ stencil[start - 2 : min(total, stop + 2), start:stop]
    if stop < total:
        weight = np.cumprod(inverse.up[start:stop][::-1])[::-1]
        from_high[1 + order] = weight
        beyond = inverse.diagonal[stop - 2] / weight[-2]
        gap = inverse.diagonal[stop - 2] * inverse.down[stop - 1] - weight[-1] * beyond
        from_high[0, -1] = gap * stencil[stop - 2, stop]
        row = row_of(lower, upper, stop - 1, max(0, start - 2), stop)
        weight = np.array([inverse.down[stop], inverse.down[stop] * inverse.down[stop + 1]])
        v = np.concatenate(
            [row, [inverse.diagonal[stop] / weight[0], inverse.diagonal[stop + 1] / weight[1]]]
        )
        to_high = v @ stencil[max(0, start - 2) : stop + 2, start:stop]
    return own, from_low, from_high, to_high, to_low


def row_of(lower, upper, i, first, last):
    turned = Inverse(np.append(0.0, upper[:-1]), np.append(lower[1:], 0.0))
    return turned.column(i, first, last)


def line_tables(total, walls, start, rows, even):
    orders = [block_operator(total, order, walls, start, rows) for order in (0, 1)]
    own = np.stack([item[0] for item in orders])
    low = np.stack([item[1] for item in orders])
    high = np.stack([item[2] for item in orders])
    edge_high = np.zeros(rows)
    edge_high[-1] = 1.0
    edge_low = np.zeros(rows)
    edge_low[0] = 1.0
    to_high = np.stack([edge_high, orders[0][3], orders[1][3]])
    to_low = np.stack([edge_low, orders[0][4], orders[1][4]])
    received = np.concatenate([high, low] if even else [low, high], axis=1)
    return own, np.repeat(received, GROUP, axis=1), np.concatenate([to_high, to_low])


def halves(values):
    high = values.astype(BF16)
    low = (values - high.astype(np.float64)).astype(BF16)
    return high, low


def split(values):
    high = values.astype(BF16)
    low = (values - high.astype(F32)).astype(BF16)
    return high, low


def sum_rows(stacked, concatenate):
    half = EDGES // 2
    return concatenate([stacked[GROUP:half], stacked[half + GROUP :]])


def x_tables(rows):
    mains = []
    for even in (True, False):
        own, received, sent = line_tables(5 * rows, False, 2 * rows, rows, even)
        scale = np.array([-1.0, VISCOSITY])[:, None, None]
        high, low = halves((own * scale).reshape(2 * rows, rows))
        edge, rest = halves((received * scale).transpose(1, 0, 2).reshape(EDGES, 2 * rows))
        edge = np.concatenate([edge, edge, sum_rows(rest, np.concatenate)]).T
        mains.append(np.concatenate([high, high, low, edge], axis=1))
    sums = np.delete(sent, [0, KINDS], axis=0).astype(np.float32)
    return np.repeat(sums[:, :, None], rows, axis=2), np.stack(mains)


def y_tables(parts, rows):
    mains, edges = [], []
    for part, even in ((0, True), (2, True), (3, False), (parts - 1, False)):
        own, received, sent = line_tables(parts * rows, True, part * rows, rows, even)
        mains.append(np.concatenate([own[0].T, own[1].T], axis=1))
        edges.append(np.concatenate([received[0], received[1]], axis=1))
        if part == 2:
            high, low = halves(np.repeat(sent, GROUP, axis=0))
            pad = np.zeros((rows // 2 - EDGES, 2 * rows), high.dtype)
            upper = np.concatenate([high, high], axis=1)
            lower = np.concatenate([low, 0 * low], axis=1)
            sums = np.concatenate([upper, pad, lower, pad]).T
    return sums, np.stack(mains).astype(np.float32), np.stack(edges).astype(np.float32)


def y_edge_kernel(
    chunk,
    field_hbm,
    y_hbm,
    x_hbm,
    x_main_hbm,
    y_main_hbm,
    y_edge_hbm,
    y1_ref,
    y2_ref,
    field_ref,
    x_ref,
    x_main_ref,
    y_main_ref,
    y_edge_ref,
    y_ref,
    acc,
    field_sems,
    table_sems,
):
    parts, planes, rows, _ = field_ref.shape
    x_odd = lax.axis_index("gx") % 2
    y_index = lax.axis_index("gy")
    y_odd = y_index % 2
    last = lax.axis_size("gy") - 1
    kind = jnp.where(y_index == 0, 0, jnp.where(y_index == last, 3, 1 + y_odd))
    sums = pltpu.make_async_copy(y_hbm, y_ref, table_sems.at[0])
    sums.start()
    fetches = []
    for i in range(planes // chunk):
        place = pl.ds(i * chunk, chunk)
        fetches.append(
            pltpu.make_async_copy(
                field_hbm.at[:, place], field_ref.at[:, place], field_sems.at[i]
            )
        )
        fetches[-1].start()
    tables = [
        pltpu.make_async_copy(x_hbm, x_ref, table_sems.at[1]),
        pltpu.make_async_copy(y_main_hbm.at[kind], y_main_ref, table_sems.at[2]),
        pltpu.make_async_copy(y_edge_hbm.at[kind], y_edge_ref, table_sems.at[3]),
        pltpu.make_async_copy(x_main_hbm.at[x_odd], x_main_ref, table_sems.at[4]),
    ]
    for copy in tables:
        copy.start()
    sums.wait()

    lane = lax.broadcasted_iota(jnp.int32, (rows, rows), 1) % GROUP
    half = EDGES // 2
    for i, fetch in enumerate(fetches):
        fetch.wait()
        blocks = []
        for part in range(parts):
            for z in range(i * chunk, (i + 1) * chunk):
                blocks.append(jnp.concatenate(split(field_ref[part, z]), axis=1))
        middle = len(blocks) // 2
        found = [
            jnp.dot(jnp.concatenate(some), y_ref[...], preferred_element_type=F32)
            for some in (blocks[:middle], blocks[middle:])
        ]
        base = i * chunk % GROUP
        for part in range(parts):
            value = None if base == 0 else acc[part]
            for z in range(chunk):
                side, place = divmod(part * chunk + z, middle)
                piece = found[side][place * rows : (place + 1) * rows]
                value = piece if value is None else jnp.where(lane == base + z, piece, value)
            if base + chunk < GROUP:
                acc[part] = value
                continue
            turned = value.T
            turned = turned[:EDGES] + turned[rows // 2 : rows // 2 + EDGES]
            to_high, to_low = turned[:half], turned[half:]
            first = jnp.where(y_odd == 0, to_high, to_low)
            second = jnp.where(y_odd == 0, to_low, to_high)
            target = slice((i + 1) * chunk - GROUP, (i + 1) * chunk)
            for kind in range(KINDS):
                tile = slice(kind * GROUP, (kind + 1) * GROUP)
                y1_ref[kind, part, target] = first[tile]
                y2_ref[kind, part, target] = second[tile]
    for copy in tables:
        copy.wait()


def x_edge_kernel(chunk, spans, field_ref, x_ref, x1_ref, x2_ref, acc):
    parts, planes, rows, lanes = field_ref.shape
    x_odd = lax.axis_index("gx") % 2

    def body(i, carry):
        part = i // (planes // chunk)
        start = lax.rem(i, planes // chunk) * chunk
        sums = [[None] * chunk for _ in spans]
        for tile in range(0, rows, GROUP):
            place = slice(tile, tile + GROUP)
            cells = [field_ref[part, start + z, place] for z in range(chunk)]
            for which, (first, last) in enumerate(spans):
                if first <= tile < last:
                    weight = x_ref[which, place]
                    for z in range(chunk):
                        term = weight * cells[z]
                        old = sums[which][z]
                        sums[which][z] = term if old is None else old + term
        for z in range(chunk):
            row = pl.ds(start + z, 1)
            for which in range(4):
                direction, order = divmod(which, 2)
                acc[direction, 1 + order, part, row] = jnp.sum(
                    sums[which][z], axis=0, keepdims=True
                )
            acc[0, 0, part, row] = field_ref[part, start + z, rows - 1 : rows]
            acc[1, 0, part, row] = field_ref[part, start + z, 0:1]
        return carry

    lax.fori_loop(0, parts * planes // chunk, body, 0)
    x1_ref[...] = acc[x_odd]
    x2_ref[...] = acc[1 - x_odd]


def spans_of(weights):
    spans = []
    for values in weights[:, :, 0]:
        rows = np.flatnonzero(np.abs(values) >= np.finfo(np.float32).tiny)
        spans.append((rows[0] // GROUP * GROUP, -(-(rows[-1] + 1) // GROUP) * GROUP))
    return tuple((int(first), int(last)) for first, last in spans)


def stack_edges(first_ref, second_ref, part, group):
    place = pl.ds(pl.multiple_of(group * GROUP, GROUP), GROUP)
    values = jnp.concatenate(
        [ref[kind, part, place] for ref in (first_ref, second_ref) for kind in range(KINDS)]
    )
    high = values.astype(BF16).astype(F32)
    return jnp.concatenate([high, values - high, sum_rows(high, jnp.concatenate)])


def wall_normal_kernel(
    depth, field_ref, second_ref, first_ref, main_ref, edge_ref, m_ref, curve_ref, out_ref, w_ref
):
    parts, planes, rows, _ = field_ref.shape
    m = m_ref[...]
    curve = curve_ref[...]

    def scaled(table):
        one = table[:, :rows]
        two = table[:, rows:]
        return jnp.concatenate([one * -m, VISCOSITY * (two * (m * m) + one * curve)], axis=1)

    high, low = split(scaled(main_ref[...]))
    edge, rest = split(scaled(edge_ref[...]))
    rest = sum_rows(rest, jnp.concatenate)
    w_ref[...] = jnp.concatenate([high, high, low, edge, edge, rest])
    lane = lax.broadcasted_iota(jnp.int32, (rows, rows), 1) % GROUP

    def body(i, carry):
        start = i * depth
        base = lax.rem(start, GROUP)
        blocks = []
        for part in range(parts):
            edges = stack_edges(first_ref, second_ref, part, start // GROUP).T
            for z in range(depth):
                high, low = split(field_ref[part, start + z])
                edge = jnp.where(lane == base + z, edges, 0.0).astype(BF16)
                blocks.append(jnp.concatenate([high, low, high, edge], axis=1))
        sums = jnp.dot(jnp.concatenate(blocks), w_ref[...], preferred_element_type=F32)
        for part in range(parts):
            for z in range(depth):
                piece = sums[(part * depth + z) * rows : (part * depth + z + 1) * rows]
                normal = field_ref[1, start + z]
                out_ref[part, start + z] = normal * piece[:, :rows] + piece[:, rows:]
        return carry

    lax.fori_loop(0, planes // depth, body, 0)


def streamwise_kernel(
    depth, field_ref, second_ref, first_ref, main_ref, add_ref, out_hbm, out_ref, sems
):
    parts, planes, rows, _ = field_ref.shape
    row = lax.broadcasted_iota(jnp.int32, (rows, rows), 0) % GROUP
    copies = []
    for start in range(0, planes, depth):
        for part in range(parts):
            edges = stack_edges(first_ref, second_ref, part, start // GROUP)
            blocks = []
            for z in range(start, start + depth):
                high, low = split(field_ref[part, z])
                edge = jnp.where(row == z % GROUP, edges, 0.0).astype(BF16)
                blocks.append(jnp.concatenate([high, low, high, edge]))
            sums = jnp.dot(
                main_ref[...], jnp.concatenate(blocks, axis=1), preferred_element_type=F32
            )
            for z in range(start, start + depth):
                piece = sums[:, (z - start) * rows : (z - start + 1) * rows]
                out_ref[part, z] = field_ref[0, z] * piece[:rows] + piece[rows:] + add_ref[part, z]
            place = pl.ds(start, depth)
            copies.append(
                pltpu.make_async_copy(
                    out_ref.at[part, place], out_hbm.at[part, place], sems.at[len(copies)]
                )
            )
            copies[-1].start()
    for copy in copies:
        copy.wait()


def exchange(first, second, axis, count, periodic):
    pairs = [(i, i + 1) for i in range(0, count, 2)]
    first = lax.ppermute(first, axis, [p for a, b in pairs for p in ((a, b), (b, a))])
    pairs = [(i, (i + 1) % count) for i in range(1, count if periodic else count - 1, 2)]
    second = lax.ppermute(second, axis, [p for a, b in pairs for p in ((a, b), (b, a))])
    return first, second


CHUNK = 4
X_CHUNK = 4
DEPTH = 8
OUT_DEPTH = 4


def on_device(x_parts, y_parts, velocity, metric_first, metric_curve):
    parts, planes, rows, _ = velocity.shape
    x_sums, x_main = x_tables(rows)
    y_sums, y_main, y_edge = y_tables(y_parts, rows)
    vmem = pl.BlockSpec(memory_space=pltpu.VMEM)
    outside = pl.BlockSpec(memory_space=pltpu.HBM)
    edge_shape = (KINDS, parts, planes, rows)
    params = pltpu.CompilerParams(vmem_limit_bytes=16 << 20)

    y1, y2, field, x_sums_, x_main, y_main, y_edge = pl.pallas_call(
        functools.partial(y_edge_kernel, CHUNK),
        out_shape=[
            pltpu.VMEM(edge_shape, F32),
            pltpu.VMEM(edge_shape, F32),
            pltpu.VMEM(velocity.shape, F32),
            pltpu.VMEM(x_sums.shape, F32),
            pltpu.VMEM(x_main.shape[1:], BF16),
            pltpu.VMEM(y_main.shape[1:], F32),
            pltpu.VMEM(y_edge.shape[1:], F32),
        ],
        in_specs=[outside] * 6,
        out_specs=[vmem] * 7,
        scratch_shapes=[
            pltpu.VMEM(y_sums.shape, BF16),
            pltpu.VMEM((parts, rows, rows), F32),
            pltpu.SemaphoreType.DMA((planes // CHUNK,)),
            pltpu.SemaphoreType.DMA((5,)),
        ],
        compiler_params=params,
        name="y_edges",
    )(*[
        pltpu.with_memory_space_constraint(item, pltpu.HBM)
        for item in (velocity, y_sums, x_sums, x_main, y_main, y_edge)
    ])
    y1, y2 = exchange(y1, y2, "gy", y_parts, False)

    x1, x2 = pl.pallas_call(
        functools.partial(x_edge_kernel, X_CHUNK, spans_of(x_sums)),
        out_shape=[pltpu.VMEM(edge_shape, F32)] * 2,
        in_specs=[vmem] * 2,
        out_specs=[vmem] * 2,
        scratch_shapes=[pltpu.VMEM((2,) + edge_shape, F32)],
        compiler_params=params,
        name="x_edges",
    )(field, x_sums_)
    x1, x2 = exchange(x1, x2, "gx", x_parts, True)

    partial = pl.pallas_call(
        functools.partial(wall_normal_kernel, DEPTH),
        out_shape=pltpu.VMEM(velocity.shape, F32),
        in_specs=[vmem] * 7,
        out_specs=vmem,
        scratch_shapes=[pltpu.VMEM((4 * rows, 2 * rows), BF16)],
        compiler_params=params,
        name="wall_normal",
    )(field, y2, y1, y_main, y_edge, metric_first[None], metric_curve[None])

    return pl.pallas_call(
        functools.partial(streamwise_kernel, OUT_DEPTH),
        out_shape=jax.ShapeDtypeStruct(velocity.shape, F32),
        in_specs=[vmem] * 5,
        out_specs=outside,
        scratch_shapes=[
            pltpu.VMEM(velocity.shape, F32),
            pltpu.SemaphoreType.DMA((parts * planes // OUT_DEPTH,)),
        ],
        compiler_params=params,
        name="streamwise",
    )(field, x2, x1, x_main, partial)


def solution(mesh):
    placed = (P(None, None, "gx", "gy"), P("gy"), P("gy"))
    return jax.shard_map(
        functools.partial(on_device, mesh.shape["gx"], mesh.shape["gy"]),
        mesh=mesh,
        in_specs=placed,
        out_specs=P(None, None, "gx", "gy"),
        check_vma=False,
    )
```

```python
import functools

import jax
import jax.numpy as jnp
import numpy as np
from jax import lax
from jax.experimental import pallas as pl
from jax.experimental.pallas import tpu as pltpu
from jax.sharding import PartitionSpec as P


VISCOSITY = 0.1
F32 = jnp.float32
BF16 = jnp.bfloat16
GROUP = 8
KINDS = 3
EDGES = 2 * KINDS * GROUP


def coefficients(total, order, walls):
    alpha = 1.0 / 3.0 if order == 0 else 2.0 / 11.0
    lower = np.full(total, alpha)
    upper = np.full(total, alpha)
    lower[0] = 0.0
    upper[total - 1] = 0.0
    if walls:
        end = 2.0 if order == 0 else 0.0
        near = 0.25 if order == 0 else 0.1
        upper[0] = end
        lower[total - 1] = end
        for row in (1, total - 2):
            lower[row] = near
            upper[row] = near
    return lower, upper


def stencil_matrix(total, order, walls):
    matrix = np.zeros((total, total))
    if order == 0:
        taps = {1: 7.0 / 9.0, -1: -7.0 / 9.0, 2: 1.0 / 36.0, -2: -1.0 / 36.0}
    else:
        near, far = 12.0 / 11.0, 3.0 / 44.0
        taps = {0: -2.0 * (near + far), 1: near, -1: near, 2: far, -2: far}
    for offset, value in taps.items():
        rows = np.arange(max(0, -offset), total - max(0, offset))
        matrix[rows, rows + offset] = value
    if walls:
        matrix[[0, 1, -2, -1]] = 0.0
        if order == 0:
            matrix[0, :3] = [-2.5, 2.0, 0.5]
            matrix[1, :3] = [-0.75, 0.0, 0.75]
            matrix[-2, -3:] = [-0.75, 0.0, 0.75]
            matrix[-1, -3:] = [-0.5, -2.0, 2.5]
        else:
            matrix[0, :4] = [2.0, -5.0, 4.0, -1.0]
            matrix[1, :3] = [1.2, -2.4, 1.2]
            matrix[-2, -3:] = [1.2, -2.4, 1.2]
            matrix[-1, -4:] = [-1.0, 4.0, -5.0, 2.0]
    return matrix


class Inverse:
    def __init__(self, lower, upper):
        total = len(lower)
        self.down = np.zeros(total + 1)
        self.up = np.zeros(total + 1)
        low = np.zeros(total + 1)
        for i in range(total - 1, -1, -1):
            low[i] = lower[i] / (1.0 - upper[i] * low[i + 1])
        high = np.zeros(total + 1)
        for i in range(total):
            high[i] = upper[i] / (1.0 - lower[i] * high[i - 1])
        self.down[:total] = -low[:total]
        self.up[:total] = -high[:total]
        self.diagonal = np.array(
            [1.0 / (1.0 - lower[i] * high[i - 1] - upper[i] * low[i + 1]) for i in range(total)]
        )

    def column(self, j, first, last):
        values = np.zeros(last - first)
        value = self.diagonal[j]
        if first <= j < last:
            values[j - first] = value
        for i in range(j + 1, last):
            value = value * self.down[i]
            if i >= first:
                values[i - first] = value
        value = self.diagonal[j]
        for i in range(j - 1, first - 1, -1):
            value = value * self.up[i]
            if i < last:
                values[i - first] = value
        return values


def block_operator(total, order, walls, start, rows):
    lower, upper = coefficients(total, order, walls)
    inverse = Inverse(lower, upper)
    stencil = stencil_matrix(total, order, walls)
    stop = start + rows
    first, last = max(0, start - 2), min(total, stop + 2)
    columns = np.stack([inverse.column(j, start, stop) for j in range(first, last)], axis=1)
    own = columns @ stencil[first:last, start:stop]
    from_low = np.zeros((KINDS, rows))
    from_high = np.zeros((KINDS, rows))
    to_high = np.zeros(rows)
    to_low = np.zeros(rows)
    if start > 0:
        weight = np.cumprod(inverse.down[start:stop])
        from_low[1 + order] = weight
        beyond = inverse.diagonal[start + 1] / weight[1]
        gap = inverse.diagonal[start + 1] * inverse.up[start] - weight[0] * beyond
        from_low[0, 0] = gap * stencil[start + 1, start - 1]
        row = row_of(lower, upper, start, start, stop)
        weight = np.array([inverse.up[start - 1], inverse.up[start - 1] * inverse.up[start - 2]])
        q = np.concatenate(
            [
                [inverse.diagonal[start - 2] / weight[1], inverse.diagonal[start - 1] / weight[0]],
                row,
                row_of(lower, upper, start, stop, min(total, stop + 2)),
            ]
        )
        to_low = q @ stencil[start - 2 : min(total, stop + 2), start:stop]
    if stop < total:
        weight = np.cumprod(inverse.up[start:stop][::-1])[::-1]
        from_high[1 + order] = weight
        beyond = inverse.diagonal[stop - 2] / weight[-2]
        gap = inverse.diagonal[stop - 2] * inverse.down[stop - 1] - weight[-1] * beyond
        from_high[0, -1] = gap * stencil[stop - 2, stop]
        row = row_of(lower, upper, stop - 1, max(0, start - 2), stop)
        weight = np.array([inverse.down[stop], inverse.down[stop] * inverse.down[stop + 1]])
        v = np.concatenate(
            [row, [inverse.diagonal[stop] / weight[0], inverse.diagonal[stop + 1] / weight[1]]]
        )
        to_high = v @ stencil[max(0, start - 2) : stop + 2, start:stop]
    return own, from_low, from_high, to_high, to_low


def row_of(lower, upper, i, first, last):
    turned = Inverse(np.append(0.0, upper[:-1]), np.append(lower[1:], 0.0))
    return turned.column(i, first, last)


def line_tables(total, walls, start, rows, even):
    orders = [block_operator(total, order, walls, start, rows) for order in (0, 1)]
    own = np.stack([item[0] for item in orders])
    low = np.stack([item[1] for item in orders])
    high = np.stack([item[2] for item in orders])
    edge_high = np.zeros(rows)
    edge_high[-1] = 1.0
    edge_low = np.zeros(rows)
    edge_low[0] = 1.0
    to_high = np.stack([edge_high, orders[0][3], orders[1][3]])
    to_low = np.stack([edge_low, orders[0][4], orders[1][4]])
    received = np.concatenate([high, low] if even else [low, high], axis=1)
    return own, np.repeat(received, GROUP, axis=1), np.concatenate([to_high, to_low])


def halves(values):
    high = values.astype(BF16)
    low = (values - high.astype(np.float64)).astype(BF16)
    return high, low


def split(values):
    high = values.astype(BF16)
    low = (values - high.astype(F32)).astype(BF16)
    return high, low


def sum_rows(stacked, concatenate):
    half = EDGES // 2
    return concatenate([stacked[GROUP:half], stacked[half + GROUP :]])


def x_tables(rows):
    mains = []
    for even in (True, False):
        own, received, sent = line_tables(5 * rows, False, 2 * rows, rows, even)
        scale = np.array([-1.0, VISCOSITY])[:, None, None]
        high, low = halves((own * scale).reshape(2 * rows, rows))
        edge, rest = halves((received * scale).transpose(1, 0, 2).reshape(EDGES, 2 * rows))
        edge = np.concatenate([edge, edge, sum_rows(rest, np.concatenate)]).T
        mains.append(np.concatenate([high, high, low, edge], axis=1))
    sums = np.delete(sent, [0, KINDS], axis=0).astype(np.float32)
    return np.repeat(sums[:, :, None], rows, axis=2), np.stack(mains)


def y_tables(parts, rows):
    mains, edges = [], []
    for part, even in ((0, True), (2, True), (3, False), (parts - 1, False)):
        own, received, sent = line_tables(parts * rows, True, part * rows, rows, even)
        mains.append(np.concatenate([own[0].T, own[1].T], axis=1))
        edges.append(np.concatenate([received[0], received[1]], axis=1))
        if part == 2:
            high, low = halves(np.repeat(sent, GROUP, axis=0))
            pad = np.zeros((rows // 2 - EDGES, 2 * rows), high.dtype)
            upper = np.concatenate([high, high], axis=1)
            lower = np.concatenate([low, 0 * low], axis=1)
            sums = np.concatenate([upper, pad, lower, pad]).T
    return sums, np.stack(mains).astype(np.float32), np.stack(edges).astype(np.float32)


def edge_kernel(
    chunk,
    spans,
    field_hbm,
    y_hbm,
    x_hbm,
    x_main_hbm,
    y_main_hbm,
    y_edge_hbm,
    x1_ref,
    x2_ref,
    y1_ref,
    y2_ref,
    field_ref,
    x_main_ref,
    y_main_ref,
    y_edge_ref,
    x_ref,
    y_ref,
    x_acc,
    acc,
    field_sems,
    table_sems,
):
    parts, planes, rows, _ = field_ref.shape
    x_odd = lax.axis_index("gx") % 2
    y_index = lax.axis_index("gy")
    y_odd = y_index % 2
    last = lax.axis_size("gy") - 1
    kind = jnp.where(y_index == 0, 0, jnp.where(y_index == last, 3, 1 + y_odd))
    sums = [
        pltpu.make_async_copy(y_hbm, y_ref, table_sems.at[0]),
        pltpu.make_async_copy(x_hbm, x_ref, table_sems.at[1]),
    ]
    fetches = []
    for i in range(planes // chunk):
        place = pl.ds(i * chunk, chunk)
        fetches.append(
            pltpu.make_async_copy(
                field_hbm.at[:, place], field_ref.at[:, place], field_sems.at[i]
            )
        )
        fetches[-1].start()
        if i == 0:
            for copy in sums:
                copy.start()
    tables = [
        pltpu.make_async_copy(y_main_hbm.at[kind], y_main_ref, table_sems.at[2]),
        pltpu.make_async_copy(y_edge_hbm.at[kind], y_edge_ref, table_sems.at[3]),
        pltpu.make_async_copy(x_main_hbm.at[x_odd], x_main_ref, table_sems.at[4]),
    ]
    for copy in tables:
        copy.start()
    for copy in sums:
        copy.wait()

    lane = lax.broadcasted_iota(jnp.int32, (rows, rows), 1) % GROUP
    half = EDGES // 2
    for i, fetch in enumerate(fetches):
        fetch.wait()
        blocks = []
        for part in range(parts):
            for z in range(i * chunk, (i + 1) * chunk):
                blocks.append(jnp.concatenate(split(field_ref[part, z]), axis=1))
        middle = len(blocks) // 2
        found = [
            jnp.dot(jnp.concatenate(some), y_ref[...], preferred_element_type=F32)
            for some in (blocks[:middle], blocks[middle:])
        ]
        for part in range(parts):
            x_sums_into(x_acc, field_ref, x_ref, spans, part, range(i * chunk, (i + 1) * chunk))
        base = i * chunk % GROUP
        for part in range(parts):
            value = None if base == 0 else acc[part]
            for z in range(chunk):
                side, place = divmod(part * chunk + z, middle)
                piece = found[side][place * rows : (place + 1) * rows]
                value = piece if value is None else jnp.where(lane == base + z, piece, value)
            if base + chunk < GROUP:
                acc[part] = value
                continue
            turned = value.T
            turned = turned[:EDGES] + turned[rows // 2 : rows // 2 + EDGES]
            to_high, to_low = turned[:half], turned[half:]
            first = jnp.where(y_odd == 0, to_high, to_low)
            second = jnp.where(y_odd == 0, to_low, to_high)
            target = slice((i + 1) * chunk - GROUP, (i + 1) * chunk)
            for kind in range(KINDS):
                tile = slice(kind * GROUP, (kind + 1) * GROUP)
                y1_ref[kind, part, target] = first[tile]
                y2_ref[kind, part, target] = second[tile]
    x1_ref[...] = x_acc[x_odd]
    x2_ref[...] = x_acc[1 - x_odd]
    for copy in tables:
        copy.wait()


def x_sums_into(acc, field_ref, x_ref, spans, part, planes):
    rows = field_ref.shape[2]
    sums = [[None] * len(planes) for _ in spans]
    for tile in range(0, rows, GROUP):
        place = slice(tile, tile + GROUP)
        cells = [field_ref[part, z, place] for z in planes]
        for which, (first, last) in enumerate(spans):
            if first <= tile < last:
                weight = x_ref[which, place]
                for i, cell in enumerate(cells):
                    old = sums[which][i]
                    sums[which][i] = weight * cell if old is None else old + weight * cell
    for i, z in enumerate(planes):
        for which in range(len(spans)):
            direction, order = divmod(which, 2)
            acc[direction, 1 + order, part, z : z + 1] = jnp.sum(
                sums[which][i], axis=0, keepdims=True
            )
        acc[0, 0, part, z : z + 1] = field_ref[part, z, rows - 1 : rows]
        acc[1, 0, part, z : z + 1] = field_ref[part, z, 0:1]


def spans_of(weights):
    spans = []
    for values in weights[:, :, 0]:
        rows = np.flatnonzero(np.abs(values) >= np.finfo(np.float32).tiny)
        spans.append((rows[0] // GROUP * GROUP, -(-(rows[-1] + 1) // GROUP) * GROUP))
    return tuple((int(first), int(last)) for first, last in spans)


def stack_edges(first_ref, second_ref, part, group):
    place = pl.ds(pl.multiple_of(group * GROUP, GROUP), GROUP)
    values = jnp.concatenate(
        [ref[kind, part, place] for ref in (first_ref, second_ref) for kind in range(KINDS)]
    )
    high = values.astype(BF16).astype(F32)
    return jnp.concatenate([high, values - high, sum_rows(high, jnp.concatenate)])


def own_kernel(
    depth, field_ref, x_main_ref, main_ref, edge_ref, m_ref, curve_ref, out_ref, rest_ref, w_ref
):
    parts, planes, rows, _ = field_ref.shape
    m = m_ref[...]
    curve = curve_ref[...]

    def scaled(table):
        one = table[:, :rows]
        two = table[:, rows:]
        return jnp.concatenate([one * -m, VISCOSITY * (two * (m * m) + one * curve)], axis=1)

    high, low = split(scaled(main_ref[...]))
    edge, rest = split(scaled(edge_ref[...]))
    rest = sum_rows(rest, jnp.concatenate)
    w_ref[...] = jnp.concatenate([high, high])
    rest_ref[...] = jnp.concatenate([low, edge, edge, rest])

    def body(i, carry):
        start = i * depth
        for part in range(parts):
            halved = [split(field_ref[part, start + z]) for z in range(depth)]
            x_sums = jnp.dot(
                x_main_ref[:, : 2 * rows],
                jnp.concatenate([jnp.concatenate(pair) for pair in halved], axis=1),
                preferred_element_type=F32,
            )
            y_sums = jnp.dot(
                jnp.concatenate([jnp.concatenate(pair, axis=1) for pair in halved]),
                w_ref[...],
                preferred_element_type=F32,
            )
            for z in range(depth):
                x_piece = x_sums[:, z * rows : (z + 1) * rows]
                y_piece = y_sums[z * rows : (z + 1) * rows]
                out_ref[part, start + z] = (
                    field_ref[0, start + z] * x_piece[:rows]
                    + field_ref[1, start + z] * y_piece[:, :rows]
                    + (x_piece[rows:] + y_piece[:, rows:])
                )
        return carry

    lax.fori_loop(0, planes // depth, body, 0)


def wall_normal_kernel(depth, field_ref, second_ref, first_ref, w_ref, add_ref, out_ref):
    parts, planes, rows, _ = field_ref.shape
    lane = lax.broadcasted_iota(jnp.int32, (rows, rows), 1) % GROUP

    def body(i, carry):
        start = i * depth
        base = lax.rem(start, GROUP)
        blocks = []
        for part in range(parts):
            edges = stack_edges(first_ref, second_ref, part, start // GROUP).T
            for z in range(depth):
                high = field_ref[part, start + z].astype(BF16)
                edge = jnp.where(lane == base + z, edges, 0.0).astype(BF16)
                blocks.append(jnp.concatenate([high, edge], axis=1))
        sums = jnp.dot(jnp.concatenate(blocks), w_ref[...], preferred_element_type=F32)
        for part in range(parts):
            for z in range(depth):
                piece = sums[(part * depth + z) * rows : (part * depth + z + 1) * rows]
                normal = field_ref[1, start + z]
                out_ref[part, start + z] = (
                    normal * piece[:, :rows] + piece[:, rows:] + add_ref[part, start + z]
                )
        return carry

    lax.fori_loop(0, planes // depth, body, 0)


def streamwise_kernel(
    depth, field_ref, second_ref, first_ref, main_ref, add_ref, out_hbm, out_ref, sems
):
    parts, planes, rows, _ = field_ref.shape
    row = lax.broadcasted_iota(jnp.int32, (rows, rows), 0) % GROUP
    copies = []
    for start in range(0, planes, depth):
        for part in range(parts):
            edges = stack_edges(first_ref, second_ref, part, start // GROUP)
            blocks = []
            for z in range(start, start + depth):
                high = field_ref[part, z].astype(BF16)
                edge = jnp.where(row == z % GROUP, edges, 0.0).astype(BF16)
                blocks.append(jnp.concatenate([high, edge]))
            sums = jnp.dot(
                main_ref[:, 2 * rows :],
                jnp.concatenate(blocks, axis=1),
                preferred_element_type=F32,
            )
            for z in range(start, start + depth):
                piece = sums[:, (z - start) * rows : (z - start + 1) * rows]
                out_ref[part, z] = field_ref[0, z] * piece[:rows] + piece[rows:] + add_ref[part, z]
            place = pl.ds(start, depth)
            copies.append(
                pltpu.make_async_copy(
                    out_ref.at[part, place], out_hbm.at[part, place], sems.at[len(copies)]
                )
            )
            copies[-1].start()
    for copy in copies:
        copy.wait()


def exchange(first, second, axis, count):
    pairs = [(i, i + 1) for i in range(0, count, 2)]
    first = lax.ppermute(first, axis, [p for a, b in pairs for p in ((a, b), (b, a))])
    pairs = [(i, (i + 1) % count) for i in range(1, count, 2)]
    second = lax.ppermute(second, axis, [p for a, b in pairs for p in ((a, b), (b, a))])
    return first, second


CHUNK = 8
DEPTH = 8
OUT_DEPTH = 4
OWN_DEPTH = 8


def on_device(x_parts, y_parts, velocity, metric_first, metric_curve):
    parts, planes, rows, _ = velocity.shape
    x_sums, x_main = x_tables(rows)
    y_sums, y_main, y_edge = y_tables(y_parts, rows)
    vmem = pl.BlockSpec(memory_space=pltpu.VMEM)
    outside = pl.BlockSpec(memory_space=pltpu.HBM)
    edge_shape = (KINDS, parts, planes, rows)
    params = pltpu.CompilerParams(vmem_limit_bytes=16 << 20)

    x1, x2, y1, y2, field, x_main, y_main, y_edge = pl.pallas_call(
        functools.partial(edge_kernel, CHUNK, spans_of(x_sums)),
        out_shape=[pltpu.VMEM(edge_shape, F32)] * 4
        + [
            pltpu.VMEM(velocity.shape, F32),
            pltpu.VMEM(x_main.shape[1:], BF16),
            pltpu.VMEM(y_main.shape[1:], F32),
            pltpu.VMEM(y_edge.shape[1:], F32),
        ],
        in_specs=[outside] * 6,
        out_specs=[vmem] * 8,
        scratch_shapes=[
            pltpu.VMEM(x_sums.shape, F32),
            pltpu.VMEM(y_sums.shape, BF16),
            pltpu.VMEM((2,) + edge_shape, F32),
            pltpu.VMEM((parts, rows, rows), F32),
            pltpu.SemaphoreType.DMA((planes // CHUNK,)),
            pltpu.SemaphoreType.DMA((5,)),
        ],
        compiler_params=params,
        name="edges",
    )(*[
        pltpu.with_memory_space_constraint(item, pltpu.HBM)
        for item in (velocity, y_sums, x_sums, x_main, y_main, y_edge)
    ])
    y1, y2 = exchange(y1, y2, "gy", y_parts)

    x1, x2 = exchange(x1, x2, "gx", x_parts)

    whole = pltpu.VMEM(velocity.shape, F32)
    own, y_rest = pl.pallas_call(
        functools.partial(own_kernel, OWN_DEPTH),
        out_shape=[whole, pltpu.VMEM((2 * rows, 2 * rows), BF16)],
        in_specs=[vmem] * 6,
        out_specs=[vmem] * 2,
        scratch_shapes=[pltpu.VMEM((2 * rows, 2 * rows), BF16)],
        compiler_params=params,
        name="own",
    )(field, x_main, y_main, y_edge, metric_first[None], metric_curve[None])
    partial = pl.pallas_call(
        functools.partial(wall_normal_kernel, DEPTH),
        out_shape=whole,
        in_specs=[vmem] * 5,
        out_specs=vmem,
        compiler_params=params,
        name="wall_normal",
    )(field, y2, y1, y_rest, own)

    return pl.pallas_call(
        functools.partial(streamwise_kernel, OUT_DEPTH),
        out_shape=jax.ShapeDtypeStruct(velocity.shape, F32),
        in_specs=[vmem] * 5,
        out_specs=outside,
        scratch_shapes=[
            pltpu.VMEM(velocity.shape, F32),
            pltpu.SemaphoreType.DMA((parts * planes // OUT_DEPTH,)),
        ],
        compiler_params=params,
        name="streamwise",
    )(field, x2, x1, x_main, partial)


def solution(mesh):
    placed = (P(None, None, "gx", "gy"), P("gy"), P("gy"))
    return jax.shard_map(
        functools.partial(on_device, mesh.shape["gx"], mesh.shape["gy"]),
        mesh=mesh,
        in_specs=placed,
        out_specs=P(None, None, "gx", "gy"),
        check_vma=False,
    )
```
